256 devices in a mesh: grp: 8 (over y, core), seq: 32 (over x, z).
Axes of the slice: x: 4, y: 4, z: 8, core: 2. Of those that a mesh axis runs over, the one named last changes fastest.
Arguments:
- query: bfloat16 [131072, 1024], P(('grp', 'seq')), may hold values from -6 to 6
- key_in: bfloat16 [131072, 1024], P(('grp', 'seq')), may hold values from -6 to 6
- value: bfloat16 [131072, 1024], P(('grp', 'seq')), may hold values from -6 to 6
- gate: bfloat16 [131072, 1024], P(('grp', 'seq')), may hold values from -6 to 6
- gain: float32 [1024], replicated, may hold values from 0.1 to 1.9
Outputs:
- attended: bfloat16 [131072, 1024], P(('grp', 'seq'))
The draws below stay inside these ranges and needn't reach their ends.
All inputs are finite; a program needn't handle non-finite values.
Results may differ from the reference program's by a relative error of at most 0.0046.
Values sent between devices are 32-bit elements; how exact they have to be, the bound alone decides.
No kernel may reach another device: no remote copies, remote signals or barrier semaphores. Data moves between devices by JAX's collectives and lax.ppermute only.
A program may use at most 320 MiB of HBM per device.

```python
import jax
import jax.numpy as jnp
from jax import lax

HEADS = 8
HEAD_DIM = 128
BLOCK = 256
TOKENS = 131072
FEATURES = 1024


def levels(own_key, dims, cuts, low, top_value):
    factor_of = 1.0
    for axis_at, blocks in cuts:
        heights = jax.random.uniform(jax.random.fold_in(jax.random.fold_in(own_key, 6), axis_at), (blocks,), jnp.float32, low / len(cuts), top_value / len(cuts))
        factor_of = factor_of * jnp.repeat(jnp.exp(heights), dims[axis_at] // blocks).reshape((-1,) + (1,) * (len(dims) - 1 - axis_at))
    return factor_of


def normal_values(rng, dims, scale, most, cuts=(), dtype=jnp.bfloat16):
    drawn = scale * jax.random.normal(rng, dims, jnp.float32)
    if cuts:
        drawn = drawn * levels(rng, dims, cuts, -0.22, 0.18)
    return jnp.clip(drawn, -most, most).astype(dtype)


def setup_inputs(seed: int = 0) -> dict:
    splits = jax.random.split(jax.random.key(seed), 6)
    return {
        "query": normal_values(splits[0], (TOKENS, FEATURES), 1.0, 6.0, ((0, 256),)),
        "key_in": normal_values(splits[1], (TOKENS, FEATURES), 1.0, 6.0, ((0, 256),)),
        "value": normal_values(splits[2], (TOKENS, FEATURES), 1.0, 6.0, ((0, 256),)),
        "gate": normal_values(splits[3], (TOKENS, FEATURES), 1.5, 6.0, ((0, 256),)),
        "gain": jnp.clip(1.0 + 0.18 * jax.random.normal(splits[4], (FEATURES,), jnp.float32), 0.1, 1.9),
    }


def reference(query, key_in, value, gate, gain):
    total_rows = query.shape[0]
    count = total_rows // BLOCK
    queries = jax.nn.silu(query.astype(jnp.float32)).astype(jnp.bfloat16)
    keys_act = jax.nn.silu(key_in.astype(jnp.float32)).astype(jnp.bfloat16)
    queries = queries.reshape(count, BLOCK, HEADS, HEAD_DIM)
    keys_act = keys_act.reshape(count, BLOCK, HEADS, HEAD_DIM)
    values_in = value.reshape(count, BLOCK, HEADS, HEAD_DIM)
    causal = jnp.arange(BLOCK)[:, None] >= jnp.arange(BLOCK)[None, :]

    def advance(state, block_in):
        q_part, k_part, v_part = block_in
        q_wide = q_part.astype(jnp.float32)
        k_wide = k_part.astype(jnp.float32)
        v_wide = v_part.astype(jnp.float32)
        scores = jnp.einsum('thd,shd->hts', q_wide, k_wide)
        scores = jnp.where(causal[None], scores, 0.0).astype(jnp.bfloat16)
        inner = jnp.einsum('hts,shd->thd', scores.astype(jnp.float32), v_wide)
        outer = jnp.einsum('thd,hde->the', q_wide, state, precision=lax.Precision.HIGHEST)
        block_kv = jnp.einsum('thd,the->hde', k_wide, v_wide)
        return (state + block_kv, inner + outer)
    start = jnp.zeros((HEADS, HEAD_DIM, HEAD_DIM), jnp.float32)
    final_state, mixed = lax.scan(advance, start, (queries, keys_act, values_in))
    mixed = mixed.reshape(total_rows, HEADS, HEAD_DIM)
    power = lax.optimization_barrier(jnp.mean(mixed * mixed, axis=-1, keepdims=True))
    normed = (mixed / jnp.sqrt(power + 1e-05)).reshape(total_rows, HEADS * HEAD_DIM)
    result = normed * gain[None, :] * jax.nn.sigmoid(gate.astype(jnp.float32))
    return result.astype(jnp.bfloat16)
```

```python
import functools

import jax
import jax.numpy as jnp
from jax import lax
from jax.experimental import pallas as pl
from jax.experimental.pallas import tpu as pltpu
from jax.sharding import PartitionSpec as P

HEADS = 8
HEAD_DIM = 128
BLOCK = 256
LANES = 2 * HEAD_DIM
VMEM_LIMIT = 48 * 1024 * 1024


def silu(u):
    u = u.astype(jnp.float32)
    return (u / (1.0 + jnp.exp(-u))).astype(jnp.bfloat16)


def dot(a, b, contract):
    return lax.dot_general(a, b, ((contract[0], contract[1]), ((), ())), preferred_element_type=jnp.float32)


def wide_dot(a, state):
    high = state.astype(jnp.bfloat16)
    low = (state - high.astype(jnp.float32)).astype(jnp.bfloat16)
    return dot(jnp.concatenate([a, a], axis=1), jnp.concatenate([high, low], axis=0), ((1,), (0,)))


def kv_body(key_ref, value_ref, keys_ref, first_ref, total_ref):
    count = key_ref.shape[0] // BLOCK
    for b in range(count):
        rows = pl.ds(b * BLOCK, BLOCK)
        keys = silu(key_ref[rows, :])
        keys_ref[rows, :] = keys
        for h in range(LANES // HEAD_DIM):
            cols = slice(h * HEAD_DIM, (h + 1) * HEAD_DIM)
            state = dot(keys[:, cols], value_ref[rows, cols], ((0,), (0,)))
            out = slice(h * HEAD_DIM, (h + 1) * HEAD_DIM)
            if b == 0:
                first_ref[out, :] = state
                total_ref[out, :] = state
            else:
                total_ref[out, :] = total_ref[out, :] + state


def intra_body(query_ref, keys_ref, value_ref, gate_ref, gain_ref, first_ref, queries_ref, inner_ref, scale_ref):
    row = lax.broadcasted_iota(jnp.int32, (BLOCK, BLOCK), 0)
    col = lax.broadcasted_iota(jnp.int32, (BLOCK, BLOCK), 1)
    causal = row >= col
    for b in range(query_ref.shape[0] // BLOCK):
        rows = pl.ds(b * BLOCK, BLOCK)
        queries = silu(query_ref[rows, :])
        queries_ref[rows, :] = queries
        gate = gate_ref[rows, :].astype(jnp.float32)
        scale_ref[rows, :] = gain_ref[...] / (1.0 + jnp.exp(-gate))
        for h in range(LANES // HEAD_DIM):
            cols = slice(h * HEAD_DIM, (h + 1) * HEAD_DIM)
            q = queries[:, cols]
            scores = dot(q, keys_ref[rows, cols], ((1,), (1,)))
            scores = jnp.where(causal, scores, 0.0).astype(jnp.bfloat16)
            mixed = dot(scores, value_ref[rows, cols], ((1,), (0,)))
            if b == 1:
                mixed = mixed + wide_dot(q, first_ref[cols, :])
            inner_ref[rows, cols] = mixed


def final_body(queries_ref, inner_ref, scale_ref, state_ref, out_ref):
    for h in range(LANES // HEAD_DIM):
        cols = slice(h * HEAD_DIM, (h + 1) * HEAD_DIM)
        mixed = inner_ref[:, cols] + wide_dot(queries_ref[:, cols], state_ref[cols, :])
        power = jnp.mean(mixed * mixed, axis=-1, keepdims=True)
        out_ref[:, cols] = (mixed / jnp.sqrt(power + 1e-05) * scale_ref[:, cols]).astype(jnp.bfloat16)


def total_body(place_ref, part_ref, out_ref):
    total = part_ref[0]
    for m in range(1, part_ref.shape[0]):
        total = total + part_ref[m]
    for g in range(out_ref.shape[0]):
        out_ref[g] = jnp.where(place_ref[0] < g, total, 0.0)


def prefix_body(part_ref, before_ref, out_ref):
    state = before_ref[0]
    for g in range(1, before_ref.shape[0]):
        state = state + before_ref[g]
    for m in range(part_ref.shape[0]):
        out_ref[m] = state
        if m + 1 < part_ref.shape[0]:
            state = state + part_ref[m]


def cols_spec(rows):
    return pl.BlockSpec((rows, LANES), lambda i: (0, i))


STATE_SPEC = pl.BlockSpec((LANES, HEAD_DIM), lambda i: (i, 0))
PARAMS = pltpu.CompilerParams(vmem_limit_bytes=VMEM_LIMIT)


def per_device(query, key_in, value, gate, gain, ranges, inner_ranges):
    rows, width = query.shape
    steps = width // LANES
    tokens = cols_spec(rows)
    state_shape = jax.ShapeDtypeStruct((width, HEAD_DIM), jnp.float32)
    keys, first, total = pl.pallas_call(
        kv_body,
        grid=(steps,),
        in_specs=[tokens, tokens],
        out_specs=[tokens, STATE_SPEC, STATE_SPEC],
        out_shape=[jax.ShapeDtypeStruct((rows, width), jnp.bfloat16), state_shape, state_shape],
        compiler_params=PARAMS,
        name="block_kv",
    )(key_in, value)

    piece = width // inner_ranges
    parts = lax.all_to_all(total.reshape(inner_ranges, piece, HEAD_DIM), "seq", 0, 0, tiled=True)

    queries, inner, scale = pl.pallas_call(
        intra_body,
        grid=(steps,),
        in_specs=[tokens, tokens, tokens, tokens, pl.BlockSpec((1, LANES), lambda i: (0, i)), STATE_SPEC],
        out_specs=[tokens, tokens, tokens],
        out_shape=[
            jax.ShapeDtypeStruct((rows, width), jnp.bfloat16),
            jax.ShapeDtypeStruct((rows, width), jnp.float32),
            jax.ShapeDtypeStruct((rows, width), jnp.float32),
        ],
        compiler_params=PARAMS,
        name="within_block",
    )(query, keys, value, gate, gain.reshape(1, width), first)

    place = lax.axis_index("grp").astype(jnp.int32).reshape(1)
    range_total = pl.pallas_call(
        total_body,
        in_specs=[pl.BlockSpec(memory_space=pltpu.SMEM), pl.BlockSpec(memory_space=pltpu.VMEM)],
        out_shape=jax.ShapeDtypeStruct((ranges, piece, HEAD_DIM), jnp.float32),
        compiler_params=PARAMS,
        name="range_total",
    )(place, parts)
    before = lax.all_to_all(range_total, "grp", 0, 0, tiled=True)
    states = pl.pallas_call(
        prefix_body,
        out_shape=jax.ShapeDtypeStruct(parts.shape, jnp.float32),
        compiler_params=PARAMS,
        name="prefix",
    )(parts, before)
    state = lax.all_to_all(states, "seq", 0, 0, tiled=True).reshape(width, HEAD_DIM)

    return pl.pallas_call(
        final_body,
        grid=(steps,),
        in_specs=[tokens, tokens, tokens, STATE_SPEC],
        out_specs=tokens,
        out_shape=jax.ShapeDtypeStruct((rows, width), jnp.bfloat16),
        compiler_params=PARAMS,
        name="gated_norm",
    )(queries, inner, scale, state)


def solution(mesh):
    return jax.shard_map(
        functools.partial(per_device, ranges=mesh.shape["grp"], inner_ranges=mesh.shape["seq"]),
        mesh=mesh,
        in_specs=(
            P(("grp", "seq"), None),
            P(("grp", "seq"), None),
            P(("grp", "seq"), None),
            P(("grp", "seq"), None),
            P(),
        ),
        out_specs=P(("grp", "seq"), None),
        check_vma=False,
    )
```

```python
import functools

import jax
import jax.numpy as jnp
from jax import lax
from jax.experimental import pallas as pl
from jax.experimental.pallas import tpu as pltpu
from jax.sharding import PartitionSpec as P

HEADS = 8
HEAD_DIM = 128
BLOCK = 256
LANES = 2 * HEAD_DIM


def silu(u):
    u = u.astype(jnp.float32)
    return (u / (1.0 + jnp.exp(-u))).astype(jnp.bfloat16)


def dot(a, b, contract):
    return lax.dot_general(a, b, ((contract[0], contract[1]), ((), ())), preferred_element_type=jnp.float32)


def wide_dot(a, state):
    high = state.astype(jnp.bfloat16)
    low = (state - high.astype(jnp.float32)).astype(jnp.bfloat16)
    return dot(jnp.concatenate([a, a], axis=1), jnp.concatenate([high, low], axis=0), ((1,), (0,)))


def stream(sources, targets, sems):
    pieces = []
    for i in range(sources[0].shape[1] // LANES):
        cols = pl.ds(i * LANES, LANES)
        piece = [
            pltpu.make_async_copy(source.at[:, cols], target.at[:, cols], sem.at[i])
            for source, target, sem in zip(sources, targets, sems)
        ]
        for copy in piece:
            copy.start()
        pieces.append(piece)
    return pieces


def heads_of(i):
    for h in range(i * LANES // HEAD_DIM, (i + 1) * LANES // HEAD_DIM):
        yield slice(h * HEAD_DIM, (h + 1) * HEAD_DIM)


def blocks_of(rows):
    return [slice(b * BLOCK, (b + 1) * BLOCK) for b in range(rows // BLOCK)]


def kv_body(key_hbm, value_hbm, total_ref, key_ref, value_ref, key_sem, value_sem):
    pieces = stream((key_hbm, value_hbm), (key_ref, value_ref), (key_sem, value_sem))
    for i, piece in enumerate(pieces):
        for copy in piece:
            copy.wait()
        for cols in heads_of(i):
            total_ref[cols, :] = dot(silu(key_ref[:, cols]), value_ref[:, cols], ((0,), (0,)))


def intra_body(
    query_hbm, key_hbm, value_hbm, gate_hbm, gain_ref, queries_ref, inner_ref, scale_ref,
    query_ref, key_ref, value_ref, gate_ref, query_sem, key_sem, value_sem, gate_sem,
):
    pieces = stream(
        (query_hbm, key_hbm, value_hbm, gate_hbm),
        (query_ref, key_ref, value_ref, gate_ref),
        (query_sem, key_sem, value_sem, gate_sem),
    )
    row = lax.broadcasted_iota(jnp.int32, (BLOCK, BLOCK), 0)
    col = lax.broadcasted_iota(jnp.int32, (BLOCK, BLOCK), 1)
    causal = row >= col
    for i, piece in enumerate(pieces):
        for copy in piece:
            copy.wait()
        for cols in heads_of(i):
            state = None
            for rows in blocks_of(query_hbm.shape[0]):
                q = silu(query_ref[rows, cols])
                k = silu(key_ref[rows, cols])
                v = value_ref[rows, cols]
                queries_ref[rows, cols] = q
                gate = gate_ref[rows, cols].astype(jnp.float32)
                scale_ref[rows, cols] = gain_ref[:, cols] / (1.0 + jnp.exp(-gate))
                scores = jnp.where(causal, dot(q, k, ((1,), (1,))), 0.0).astype(jnp.bfloat16)
                mixed = dot(scores, v, ((1,), (0,)))
                if state is not None:
                    mixed = mixed + wide_dot(q, state)
                inner_ref[rows, cols] = mixed
                if rows.stop < query_hbm.shape[0]:
                    block_kv = dot(k, v, ((0,), (0,)))
                    state = block_kv if state is None else state + block_kv


def final_body(queries_ref, inner_ref, scale_ref, state_ref, out_hbm, out_ref, sem):
    stores = []
    for i in range(queries_ref.shape[1] // LANES):
        for cols in heads_of(i):
            mixed = inner_ref[:, cols] + wide_dot(queries_ref[:, cols], state_ref[cols, :])
            power = jnp.mean(mixed * mixed, axis=-1, keepdims=True)
            out_ref[:, cols] = (mixed * (1.0 / jnp.sqrt(power + 1e-05)) * scale_ref[:, cols]).astype(jnp.bfloat16)
        cols = pl.ds(i * LANES, LANES)
        store = pltpu.make_async_copy(out_ref.at[:, cols], out_hbm.at[:, cols], sem.at[i])
        store.start()
        stores.append(store)
    for store in stores:
        store.wait()


def total_body(place_ref, part_ref, out_ref):
    total = part_ref[0]
    for m in range(1, part_ref.shape[0]):
        total = total + part_ref[m]
    for g in range(out_ref.shape[0]):
        out_ref[g] = jnp.where(place_ref[0] < g, total, 0.0)


def prefix_body(part_ref, before_ref, out_ref):
    state = before_ref[0]
    for g in range(1, before_ref.shape[0]):
        state = state + before_ref[g]
    for m in range(part_ref.shape[0]):
        out_ref[m] = state
        if m + 1 < part_ref.shape[0]:
            state = state + part_ref[m]


HBM = pl.BlockSpec(memory_space=pltpu.HBM)
VMEM = pl.BlockSpec(memory_space=pltpu.VMEM)


def params(mib):
    return pltpu.CompilerParams(vmem_limit_bytes=mib * 1024 * 1024)


def per_device(query, key_in, value, gate, gain, ranges, inner_ranges):
    rows, width = query.shape
    steps = width // LANES
    tokens = pltpu.VMEM((rows, width), jnp.bfloat16)
    wide_tokens = pltpu.VMEM((rows, width), jnp.float32)
    sems = pltpu.SemaphoreType.DMA((steps,))
    query, key_in, value, gate = (pltpu.with_memory_space_constraint(a, pltpu.HBM) for a in (query, key_in, value, gate))
    total = pl.pallas_call(
        kv_body,
        in_specs=[HBM, HBM],
        out_specs=VMEM,
        out_shape=jax.ShapeDtypeStruct((width, HEAD_DIM), jnp.float32),
        scratch_shapes=[tokens, tokens, sems, sems],
        compiler_params=params(16),
        name="range_part",
    )(key_in, value)

    piece = width // inner_ranges
    parts = lax.all_to_all(total.reshape(inner_ranges, piece, HEAD_DIM), "seq", 0, 0, tiled=True)

    queries, inner, scale = pl.pallas_call(
        intra_body,
        in_specs=[HBM, HBM, HBM, HBM, VMEM],
        out_specs=[VMEM] * 3,
        out_shape=[
            jax.ShapeDtypeStruct((rows, width), jnp.bfloat16),
            jax.ShapeDtypeStruct((rows, width), jnp.float32),
            jax.ShapeDtypeStruct((rows, width), jnp.float32),
        ],
        scratch_shapes=[tokens] * 4 + [sems] * 4,
        compiler_params=params(16),
        name="within_block",
    )(query, key_in, value, gate, gain.reshape(1, width))
    parts, queries, inner, scale = lax.optimization_barrier((parts, queries, inner, scale))

    place = lax.axis_index("grp").astype(jnp.int32).reshape(1)
    range_total = pl.pallas_call(
        total_body,
        in_specs=[pl.BlockSpec(memory_space=pltpu.SMEM), VMEM],
        out_specs=VMEM,
        out_shape=jax.ShapeDtypeStruct((ranges, piece, HEAD_DIM), jnp.float32),
        compiler_params=params(16),
        name="range_total",
    )(place, parts)
    before = lax.all_to_all(range_total, "grp", 0, 0, tiled=True)
    states = pl.pallas_call(
        prefix_body,
        in_specs=[VMEM, VMEM],
        out_specs=VMEM,
        out_shape=jax.ShapeDtypeStruct(parts.shape, jnp.float32),
        compiler_params=params(16),
        name="prefix",
    )(parts, before)
    state = lax.all_to_all(states, "seq", 0, 0, tiled=True).reshape(width, HEAD_DIM)

    return pl.pallas_call(
        final_body,
        in_specs=[VMEM] * 4,
        out_specs=HBM,
        out_shape=jax.ShapeDtypeStruct((rows, width), jnp.bfloat16),
        scratch_shapes=[tokens, pltpu.SemaphoreType.DMA((steps,))],
        compiler_params=params(16),
        name="gated_norm",
    )(queries, inner, scale, state)


def solution(mesh):
    return jax.shard_map(
        functools.partial(per_device, ranges=mesh.shape["grp"], inner_ranges=mesh.shape["seq"]),
        mesh=mesh,
        in_specs=(
            P(("grp", "seq"), None),
            P(("grp", "seq"), None),
            P(("grp", "seq"), None),
            P(("grp", "seq"), None),
            P(),
        ),
        out_specs=P(("grp", "seq"), None),
        check_vma=False,
    )
```

```python
import functools

import jax
import jax.numpy as jnp
from jax import lax
from jax.experimental import pallas as pl
from jax.experimental.pallas import tpu as pltpu
from jax.sharding import PartitionSpec as P

HEADS = 8
HEAD_DIM = 128
BLOCK = 256
LANES = 2 * HEAD_DIM
KV_LANES = 4 * HEAD_DIM


def silu(u):
    u = u.astype(jnp.float32)
    return (u / (1.0 + jnp.exp(-u))).astype(jnp.bfloat16)


def dot(a, b, contract):
    return lax.dot_general(a, b, ((contract[0], contract[1]), ((), ())), preferred_element_type=jnp.float32)


def wide_dot(a, state):
    high = state.astype(jnp.bfloat16)
    low = (state - high.astype(jnp.float32)).astype(jnp.bfloat16)
    return dot(jnp.concatenate([a, a], axis=1), jnp.concatenate([high, low], axis=0), ((1,), (0,)))


def stream(sources, targets, sems, lanes):
    pieces = []
    for i in range(sources[0].shape[1] // lanes):
        cols = pl.ds(i * lanes, lanes)
        piece = [
            pltpu.make_async_copy(source.at[:, cols], target.at[:, cols], sem.at[i])
            for source, target, sem in zip(sources, targets, sems)
        ]
        for copy in piece:
            copy.start()
        pieces.append(piece)
    return pieces


def heads_of(i, lanes):
    for h in range(i * lanes // HEAD_DIM, (i + 1) * lanes // HEAD_DIM):
        yield slice(h * HEAD_DIM, (h + 1) * HEAD_DIM)


def blocks_of(rows):
    return [slice(b * BLOCK, (b + 1) * BLOCK) for b in range(rows // BLOCK)]


def kv_body(key_hbm, value_hbm, total_hbm, key_ref, value_ref, total_ref, key_sem, value_sem, total_sem):
    pieces = stream((key_hbm, value_hbm), (key_ref, value_ref), (key_sem, value_sem), KV_LANES)
    stores = []
    for i, piece in enumerate(pieces):
        for copy in piece:
            copy.wait()
        for cols in heads_of(i, KV_LANES):
            total_ref[cols, :] = dot(silu(key_ref[:, cols]), value_ref[:, cols], ((0,), (0,)))
        done = pl.ds(i * KV_LANES, KV_LANES)
        store = pltpu.make_async_copy(total_ref.at[done, :], total_hbm.at[done, :], total_sem.at[i])
        store.start()
        stores.append(store)
    for store in stores:
        store.wait()


def intra_body(
    query_hbm, key_hbm, value_hbm, gate_hbm, gain_ref, queries_ref, inner_ref, scale_ref,
    query_ref, key_ref, value_ref, gate_ref, query_sem, key_sem, value_sem, gate_sem,
):
    pieces = stream(
        (query_hbm, key_hbm, value_hbm, gate_hbm),
        (query_ref, key_ref, value_ref, gate_ref),
        (query_sem, key_sem, value_sem, gate_sem),
        LANES,
    )
    row = lax.broadcasted_iota(jnp.int32, (BLOCK, BLOCK), 0)
    col = lax.broadcasted_iota(jnp.int32, (BLOCK, BLOCK), 1)
    causal = row >= col
    for i, piece in enumerate(pieces):
        for copy in piece:
            copy.wait()
        for cols in heads_of(i, LANES):
            state = None
            for rows in blocks_of(query_hbm.shape[0]):
                q = silu(query_ref[rows, cols])
                k = silu(key_ref[rows, cols])
                v = value_ref[rows, cols]
                queries_ref[rows, cols] = q
                gate = gate_ref[rows, cols].astype(jnp.float32)
                scale_ref[rows, cols] = gain_ref[:, cols] / (1.0 + jnp.exp(-gate))
                scores = jnp.where(causal, dot(q, k, ((1,), (1,))), 0.0).astype(jnp.bfloat16)
                mixed = dot(scores, v, ((1,), (0,)))
                if state is not None:
                    mixed = mixed + wide_dot(q, state)
                inner_ref[rows, cols] = mixed
                if rows.stop < query_hbm.shape[0]:
                    block_kv = dot(k, v, ((0,), (0,)))
                    state = block_kv if state is None else state + block_kv


def final_body(queries_ref, inner_ref, scale_ref, state_ref, out_hbm, out_ref, sem):
    stores = []
    for i in range(queries_ref.shape[1] // LANES):
        for cols in heads_of(i, LANES):
            mixed = inner_ref[:, cols] + wide_dot(queries_ref[:, cols], state_ref[cols, :])
            power = jnp.mean(mixed * mixed, axis=-1, keepdims=True)
            out_ref[:, cols] = (mixed * lax.rsqrt(power + 1e-05) * scale_ref[:, cols]).astype(jnp.bfloat16)
        cols = pl.ds(i * LANES, LANES)
        store = pltpu.make_async_copy(out_ref.at[:, cols], out_hbm.at[:, cols], sem.at[i])
        store.start()
        stores.append(store)
    for store in stores:
        store.wait()


def total_body(place_ref, part_ref, out_ref):
    total = part_ref[0]
    for m in range(1, part_ref.shape[0]):
        total = total + part_ref[m]
    for g in range(out_ref.shape[0]):
        out_ref[g] = jnp.where(place_ref[0] < g, total, 0.0)


def prefix_body(part_ref, before_ref, out_ref):
    state = before_ref[0]
    for g in range(1, before_ref.shape[0]):
        state = state + before_ref[g]
    for m in range(part_ref.shape[0]):
        out_ref[m] = state
        if m + 1 < part_ref.shape[0]:
            state = state + part_ref[m]


HBM = pl.BlockSpec(memory_space=pltpu.HBM)
VMEM = pl.BlockSpec(memory_space=pltpu.VMEM)


def params(mib):
    return pltpu.CompilerParams(vmem_limit_bytes=mib * 1024 * 1024)


def per_device(query, key_in, value, gate, gain, ranges, inner_ranges):
    rows, width = query.shape
    steps = width // LANES
    tokens = pltpu.VMEM((rows, width), jnp.bfloat16)
    wide_tokens = pltpu.VMEM((rows, width), jnp.float32)
    sems = pltpu.SemaphoreType.DMA((steps,))
    query, key_in, value, gate = (pltpu.with_memory_space_constraint(a, pltpu.HBM) for a in (query, key_in, value, gate))
    total = pl.pallas_call(
        kv_body,
        in_specs=[HBM, HBM],
        out_specs=HBM,
        out_shape=pltpu.HBM((width, HEAD_DIM), jnp.float32),
        scratch_shapes=[tokens, tokens, pltpu.VMEM((width, HEAD_DIM), jnp.float32)]
        + [pltpu.SemaphoreType.DMA((width // KV_LANES,))] * 3,
        compiler_params=params(16),
        name="range_part",
    )(key_in, value)

    piece = width // inner_ranges
    parts = lax.all_to_all(total.reshape(inner_ranges, piece, HEAD_DIM), "seq", 0, 0, tiled=True)

    queries, inner, scale = pl.pallas_call(
        intra_body,
        in_specs=[HBM, HBM, HBM, HBM, VMEM],
        out_specs=[VMEM] * 3,
        out_shape=[
            jax.ShapeDtypeStruct((rows, width), jnp.bfloat16),
            jax.ShapeDtypeStruct((rows, width), jnp.float32),
            jax.ShapeDtypeStruct((rows, width), jnp.float32),
        ],
        scratch_shapes=[tokens] * 4 + [sems] * 4,
        compiler_params=params(16),
        name="within_block",
    )(query, key_in, value, gate, gain.reshape(1, width))
    parts, queries, inner, scale = lax.optimization_barrier((parts, queries, inner, scale))

    place = lax.axis_index("grp").astype(jnp.int32).reshape(1)
    range_total = pl.pallas_call(
        total_body,
        in_specs=[pl.BlockSpec(memory_space=pltpu.SMEM), VMEM],
        out_specs=VMEM,
        out_shape=jax.ShapeDtypeStruct((ranges, piece, HEAD_DIM), jnp.float32),
        compiler_params=params(16),
        name="range_total",
    )(place, parts)
    before = lax.all_to_all(range_total, "grp", 0, 0, tiled=True)
    states = pl.pallas_call(
        prefix_body,
        in_specs=[VMEM, VMEM],
        out_specs=VMEM,
        out_shape=jax.ShapeDtypeStruct(parts.shape, jnp.float32),
        compiler_params=params(16),
        name="prefix",
    )(parts, before)
    state = lax.all_to_all(states, "seq", 0, 0, tiled=True).reshape(width, HEAD_DIM)

    return pl.pallas_call(
        final_body,
        in_specs=[VMEM] * 4,
        out_specs=HBM,
        out_shape=jax.ShapeDtypeStruct((rows, width), jnp.bfloat16),
        scratch_shapes=[tokens, pltpu.SemaphoreType.DMA((steps,))],
        compiler_params=params(16),
        name="gated_norm",
    )(queries, inner, scale, state)


def solution(mesh):
    return jax.shard_map(
        functools.partial(per_device, ranges=mesh.shape["grp"], inner_ranges=mesh.shape["seq"]),
        mesh=mesh,
        in_specs=(
            P(("grp", "seq"), None),
            P(("grp", "seq"), None),
            P(("grp", "seq"), None),
            P(("grp", "seq"), None),
            P(),
        ),
        out_specs=P(("grp", "seq"), None),
        check_vma=False,
    )
```

```python
import functools

import jax
import jax.numpy as jnp
from jax import lax
from jax.experimental import pallas as pl
from jax.experimental.pallas import tpu as pltpu
from jax.sharding import PartitionSpec as P

HEADS = 8
HEAD_DIM = 128
BLOCK = 256
LANES = 2 * HEAD_DIM
KV_LANES = 4 * HEAD_DIM


def silu(u):
    u = u.astype(jnp.float32)
    return (u / (1.0 + jnp.exp(-u))).astype(jnp.bfloat16)


def dot(a, b, contract):
    return lax.dot_general(a, b, ((contract[0], contract[1]), ((), ())), preferred_element_type=jnp.float32)


def wide_dot(a, state):
    high = state.astype(jnp.bfloat16)
    low = (state - high.astype(jnp.float32)).astype(jnp.bfloat16)
    return dot(jnp.concatenate([a, a], axis=1), jnp.concatenate([high, low], axis=0), ((1,), (0,)))


def stream(sources, targets, sems, lanes):
    pieces = []
    for i in range(sources[0].shape[1] // lanes):
        cols = pl.ds(i * lanes, lanes)
        piece = [
            pltpu.make_async_copy(source.at[:, cols], target.at[:, cols], sem.at[i])
            for source, target, sem in zip(sources, targets, sems)
        ]
        for copy in piece:
            copy.start()
        pieces.append(piece)
    return pieces


def heads_of(i, lanes):
    for h in range(i * lanes // HEAD_DIM, (i + 1) * lanes // HEAD_DIM):
        yield slice(h * HEAD_DIM, (h + 1) * HEAD_DIM)


def blocks_of(rows):
    return [slice(b * BLOCK, (b + 1) * BLOCK) for b in range(rows // BLOCK)]


def kv_body(key_hbm, value_hbm, total_hbm, key_ref, value_ref, total_ref, key_sem, value_sem, total_sem):
    pieces = stream((key_hbm, value_hbm), (key_ref, value_ref), (key_sem, value_sem), KV_LANES)
    stores = []
    for i, piece in enumerate(pieces):
        for copy in piece:
            copy.wait()
        for cols in heads_of(i, KV_LANES):
            total_ref[cols, :] = dot(silu(key_ref[:, cols]), value_ref[:, cols], ((0,), (0,)))
        done = pl.ds(i * KV_LANES, KV_LANES)
        store = pltpu.make_async_copy(total_ref.at[done, :], total_hbm.at[done, :], total_sem.at[i])
        store.start()
        stores.append(store)
    for store in stores:
        store.wait()


def intra_body(
    query_hbm, key_hbm, value_hbm, gate_hbm, gain_ref, queries_ref, inner_ref, scale_ref,
    query_ref, key_ref, value_ref, gate_ref, query_sem, key_sem, value_sem, gate_sem,
):
    pieces = stream(
        (query_hbm, key_hbm, value_hbm, gate_hbm),
        (query_ref, key_ref, value_ref, gate_ref),
        (query_sem, key_sem, value_sem, gate_sem),
        LANES,
    )
    row = lax.broadcasted_iota(jnp.int32, (BLOCK, BLOCK), 0)
    col = lax.broadcasted_iota(jnp.int32, (BLOCK, BLOCK), 1)
    causal = row >= col
    for i, piece in enumerate(pieces):
        for copy in piece:
            copy.wait()
        for cols in heads_of(i, LANES):
            state = None
            for rows in blocks_of(query_hbm.shape[0]):
                q = silu(query_ref[rows, cols])
                k = silu(key_ref[rows, cols])
                v = value_ref[rows, cols]
                queries_ref[rows, cols] = q
                gate = gate_ref[rows, cols].astype(jnp.float32)
                scale_ref[rows, cols] = gain_ref[:, cols] / (1.0 + jnp.exp(-gate))
                scores = jnp.where(causal, dot(q, k, ((1,), (1,))), 0.0).astype(jnp.bfloat16)
                mixed = dot(scores, v, ((1,), (0,)))
                if state is not None:
                    mixed = mixed + wide_dot(q, state)
                inner_ref[rows, cols] = mixed
                if rows.stop < query_hbm.shape[0]:
                    block_kv = dot(k, v, ((0,), (0,)))
                    state = block_kv if state is None else state + block_kv


def final_body(queries_ref, inner_ref, scale_ref, state_ref, out_hbm, out_ref, sem):
    stores = []
    for i in range(queries_ref.shape[1] // LANES):
        for cols in heads_of(i, LANES):
            mixed = inner_ref[:, cols] + wide_dot(queries_ref[:, cols], state_ref[cols, :])
            power = jnp.mean(mixed * mixed, axis=-1, keepdims=True)
            out_ref[:, cols] = (mixed * lax.rsqrt(power + 1e-05) * scale_ref[:, cols]).astype(jnp.bfloat16)
        cols = pl.ds(i * LANES, LANES)
        store = pltpu.make_async_copy(out_ref.at[:, cols], out_hbm.at[:, cols], sem.at[i])
        store.start()
        stores.append(store)
    for store in stores:
        store.wait()


def total_body(part_ref, out_ref):
    total = part_ref[0]
    for m in range(1, part_ref.shape[0]):
        total = total + part_ref[m]
    out_ref[...] = total


def prefix_body(place_ref, part_ref, inner_ref, other_ref, *refs):
    del inner_ref
    *total_refs, out_ref = refs
    place = place_ref[0]
    state = jnp.where(place % 2 == 1, other_ref[...], 0.0)
    for pair, total_ref in enumerate(total_refs, 1):
        state = state + jnp.where((place // 2) ^ pair < place // 2, total_ref[...], 0.0)
    for m in range(part_ref.shape[0]):
        out_ref[m] = state
        if m + 1 < part_ref.shape[0]:
            state = state + part_ref[m]


HBM = pl.BlockSpec(memory_space=pltpu.HBM)
VMEM = pl.BlockSpec(memory_space=pltpu.VMEM)


def params(mib):
    return pltpu.CompilerParams(vmem_limit_bytes=mib * 1024 * 1024)


def per_device(query, key_in, value, gate, gain, ranges, inner_ranges):
    rows, width = query.shape
    steps = width // LANES
    tokens = pltpu.VMEM((rows, width), jnp.bfloat16)
    wide_tokens = pltpu.VMEM((rows, width), jnp.float32)
    sems = pltpu.SemaphoreType.DMA((steps,))
    query, key_in, value, gate = (pltpu.with_memory_space_constraint(a, pltpu.HBM) for a in (query, key_in, value, gate))
    total = pl.pallas_call(
        kv_body,
        in_specs=[HBM, HBM],
        out_specs=HBM,
        out_shape=pltpu.HBM((width, HEAD_DIM), jnp.float32),
        scratch_shapes=[tokens, tokens, pltpu.VMEM((width, HEAD_DIM), jnp.float32)]
        + [pltpu.SemaphoreType.DMA((width // KV_LANES,))] * 3,
        compiler_params=params(16),
        name="range_part",
    )(key_in, value)

    piece = width // inner_ranges
    parts = lax.all_to_all(total.reshape(inner_ranges, piece, HEAD_DIM), "seq", 0, 0, tiled=True)

    queries, inner, scale = pl.pallas_call(
        intra_body,
        in_specs=[HBM, HBM, HBM, HBM, VMEM],
        out_specs=[VMEM] * 3,
        out_shape=[
            jax.ShapeDtypeStruct((rows, width), jnp.bfloat16),
            jax.ShapeDtypeStruct((rows, width), jnp.float32),
            jax.ShapeDtypeStruct((rows, width), jnp.float32),
        ],
        scratch_shapes=[tokens] * 4 + [sems] * 4,
        compiler_params=params(16),
        name="within_block",
    )(query, key_in, value, gate, gain.reshape(1, width))
    parts, queries, inner, scale = lax.optimization_barrier((parts, queries, inner, scale))

    def swap(a, bits):
        return lax.ppermute(a, "grp", [(g, g ^ bits) for g in range(ranges)])

    place = lax.axis_index("grp").astype(jnp.int32).reshape(1)
    range_total = pl.pallas_call(
        total_body,
        in_specs=[VMEM],
        out_specs=VMEM,
        out_shape=jax.ShapeDtypeStruct((piece, HEAD_DIM), jnp.float32),
        compiler_params=params(16),
        name="range_total",
    )(parts)
    other = swap(range_total, 1)
    both = range_total + other
    totals = [swap(both, 2 * pair) for pair in range(1, ranges // 2)]
    states = pl.pallas_call(
        prefix_body,
        in_specs=[pl.BlockSpec(memory_space=pltpu.SMEM)] + [VMEM] * (3 + len(totals)),
        out_specs=VMEM,
        out_shape=jax.ShapeDtypeStruct(parts.shape, jnp.float32),
        compiler_params=params(16),
        name="prefix",
    )(place, parts, inner, other, *totals)
    state = lax.all_to_all(states, "seq", 0, 0, tiled=True).reshape(width, HEAD_DIM)

    return pl.pallas_call(
        final_body,
        in_specs=[VMEM] * 4,
        out_specs=HBM,
        out_shape=jax.ShapeDtypeStruct((rows, width), jnp.bfloat16),
        scratch_shapes=[tokens, pltpu.SemaphoreType.DMA((steps,))],
        compiler_params=params(16),
        name="gated_norm",
    )(queries, inner, scale, state)


def solution(mesh):
    return jax.shard_map(
        functools.partial(per_device, ranges=mesh.shape["grp"], inner_ranges=mesh.shape["seq"]),
        mesh=mesh,
        in_specs=(
            P(("grp", "seq"), None),
            P(("grp", "seq"), None),
            P(("grp", "seq"), None),
            P(("grp", "seq"), None),
            P(),
        ),
        out_specs=P(("grp", "seq"), None),
        check_vma=False,
    )
```

```python
import functools
import itertools

import jax
import jax.numpy as jnp
from jax import lax
from jax.experimental import pallas as pl
from jax.experimental.pallas import tpu as pltpu
from jax.sharding import Mesh
from jax.sharding import PartitionSpec as P

HEADS = 8
HEAD_DIM = 128
BLOCK = 256
LANES = 2 * HEAD_DIM
KV_LANES = 4 * HEAD_DIM
EXCHANGE_BITS = (0, 4, 3, 2, 1)


def silu(u):
    u = u.astype(jnp.float32)
    return (u / (1.0 + jnp.exp(-u))).astype(jnp.bfloat16)


def dot(a, b, contract):
    return lax.dot_general(a, b, ((contract[0], contract[1]), ((), ())), preferred_element_type=jnp.float32)


def wide_dot(a, state):
    high = state.astype(jnp.bfloat16)
    low = (state - high.astype(jnp.float32)).astype(jnp.bfloat16)
    return dot(jnp.concatenate([a, a], axis=1), jnp.concatenate([high, low], axis=0), ((1,), (0,)))


def stream(sources, targets, sems, lanes):
    pieces = []
    for i in range(sources[0].shape[1] // lanes):
        cols = pl.ds(i * lanes, lanes)
        piece = [
            pltpu.make_async_copy(source.at[:, cols], target.at[:, cols], sem.at[i])
            for source, target, sem in zip(sources, targets, sems)
        ]
        for copy in piece:
            copy.start()
        pieces.append(piece)
    return pieces


def heads_of(i, lanes):
    for h in range(i * lanes // HEAD_DIM, (i + 1) * lanes // HEAD_DIM):
        yield slice(h * HEAD_DIM, (h + 1) * HEAD_DIM)


def blocks_of(rows):
    return [slice(b * BLOCK, (b + 1) * BLOCK) for b in range(rows // BLOCK)]


def kv_body(key_hbm, value_hbm, total_hbm, key_ref, value_ref, total_ref, key_sem, value_sem, total_sem):
    pieces = stream((key_hbm, value_hbm), (key_ref, value_ref), (key_sem, value_sem), KV_LANES)
    stores = []
    for i, piece in enumerate(pieces):
        for copy in piece:
            copy.wait()
        for cols in heads_of(i, KV_LANES):
            total_ref[cols, :] = dot(silu(key_ref[:, cols]), value_ref[:, cols], ((0,), (0,)))
        done = pl.ds(i * KV_LANES, KV_LANES)
        store = pltpu.make_async_copy(total_ref.at[done, :], total_hbm.at[done, :], total_sem.at[i])
        store.start()
        stores.append(store)
    for store in stores:
        store.wait()


def intra_body(
    query_hbm, key_hbm, value_hbm, gate_hbm, gain_ref, queries_ref, inner_ref, scale_ref,
    query_ref, key_ref, value_ref, gate_ref, query_sem, key_sem, value_sem, gate_sem,
):
    pieces = stream(
        (query_hbm, key_hbm, value_hbm, gate_hbm),
        (query_ref, key_ref, value_ref, gate_ref),
        (query_sem, key_sem, value_sem, gate_sem),
        LANES,
    )
    row = lax.broadcasted_iota(jnp.int32, (BLOCK, BLOCK), 0)
    col = lax.broadcasted_iota(jnp.int32, (BLOCK, BLOCK), 1)
    causal = row >= col
    for i, piece in enumerate(pieces):
        for copy in piece:
            copy.wait()
        for cols in heads_of(i, LANES):
            state = None
            for rows in blocks_of(query_hbm.shape[0]):
                q = silu(query_ref[rows, cols])
                k = silu(key_ref[rows, cols])
                v = value_ref[rows, cols]
                queries_ref[rows, cols] = q
                gate = gate_ref[rows, cols].astype(jnp.float32)
                scale_ref[rows, cols] = gain_ref[:, cols] / (1.0 + jnp.exp(-gate))
                scores = jnp.where(causal, dot(q, k, ((1,), (1,))), 0.0).astype(jnp.bfloat16)
                mixed = dot(scores, v, ((1,), (0,)))
                if state is not None:
                    mixed = mixed + wide_dot(q, state)
                inner_ref[rows, cols] = mixed
                if rows.stop < query_hbm.shape[0]:
                    block_kv = dot(k, v, ((0,), (0,)))
                    state = block_kv if state is None else state + block_kv


def final_body(queries_ref, inner_ref, scale_ref, state_ref, out_hbm, out_ref, sem):
    stores = []
    for i in range(queries_ref.shape[1] // LANES):
        for cols in heads_of(i, LANES):
            mixed = inner_ref[:, cols] + wide_dot(queries_ref[:, cols], state_ref[cols, :])
            power = jnp.mean(mixed * mixed, axis=-1, keepdims=True)
            out_ref[:, cols] = (mixed * lax.rsqrt(power + 1e-05) * scale_ref[:, cols]).astype(jnp.bfloat16)
        cols = pl.ds(i * LANES, LANES)
        store = pltpu.make_async_copy(out_ref.at[:, cols], out_hbm.at[:, cols], sem.at[i])
        store.start()
        stores.append(store)
    for store in stores:
        store.wait()


def total_body(part_ref, out_ref):
    total = part_ref[0]
    for m in range(1, part_ref.shape[0]):
        total = total + part_ref[m]
    out_ref[...] = total


def prefix_body(order, place_ref, part_ref, inner_ref, other_ref, *refs):
    del inner_ref
    *total_refs, out_ref = refs
    place = place_ref[0]
    state = jnp.where(place % 2 == 1, other_ref[...], 0.0)
    for pair, total_ref in enumerate(total_refs, 1):
        state = state + jnp.where((place // 2) ^ pair < place // 2, total_ref[...], 0.0)
    for m in order:
        out_ref[m] = state
        if m != order[-1]:
            state = state + part_ref[m]


HBM = pl.BlockSpec(memory_space=pltpu.HBM)
VMEM = pl.BlockSpec(memory_space=pltpu.VMEM)


def params(mib):
    return pltpu.CompilerParams(vmem_limit_bytes=mib * 1024 * 1024)


def per_device(query, key_in, value, gate, gain, ranges, inner_ranges, exchange, order):
    rows, width = query.shape
    steps = width // LANES
    tokens = pltpu.VMEM((rows, width), jnp.bfloat16)
    wide_tokens = pltpu.VMEM((rows, width), jnp.float32)
    sems = pltpu.SemaphoreType.DMA((steps,))
    query, key_in, value, gate = (pltpu.with_memory_space_constraint(a, pltpu.HBM) for a in (query, key_in, value, gate))
    total = pl.pallas_call(
        kv_body,
        in_specs=[HBM, HBM],
        out_specs=HBM,
        out_shape=pltpu.HBM((width, HEAD_DIM), jnp.float32),
        scratch_shapes=[tokens, tokens, pltpu.VMEM((width, HEAD_DIM), jnp.float32)]
        + [pltpu.SemaphoreType.DMA((width // KV_LANES,))] * 3,
        compiler_params=params(16),
        name="range_part",
    )(key_in, value)

    piece = width // inner_ranges
    parts = lax.all_to_all(total.reshape(inner_ranges, piece, HEAD_DIM), exchange, 0, 0, tiled=True)

    queries, inner, scale = pl.pallas_call(
        intra_body,
        in_specs=[HBM, HBM, HBM, HBM, VMEM],
        out_specs=[VMEM] * 3,
        out_shape=[
            jax.ShapeDtypeStruct((rows, width), jnp.bfloat16),
            jax.ShapeDtypeStruct((rows, width), jnp.float32),
            jax.ShapeDtypeStruct((rows, width), jnp.float32),
        ],
        scratch_shapes=[tokens] * 4 + [sems] * 4,
        compiler_params=params(16),
        name="within_block",
    )(query, key_in, value, gate, gain.reshape(1, width))
    parts, queries, inner, scale = lax.optimization_barrier((parts, queries, inner, scale))

    def swap(a, bits):
        return lax.ppermute(a, "grp", [(g, g ^ bits) for g in range(ranges)])

    place = lax.axis_index("grp").astype(jnp.int32).reshape(1)
    range_total = pl.pallas_call(
        total_body,
        in_specs=[VMEM],
        out_specs=VMEM,
        out_shape=jax.ShapeDtypeStruct((piece, HEAD_DIM), jnp.float32),
        compiler_params=params(16),
        name="range_total",
    )(parts)
    other = swap(range_total, 1)
    both = range_total + other
    totals = [swap(both, 2 * pair) for pair in range(1, ranges // 2)]
    states = pl.pallas_call(
        functools.partial(prefix_body, order),
        in_specs=[pl.BlockSpec(memory_space=pltpu.SMEM)] + [VMEM] * (3 + len(totals)),
        out_specs=VMEM,
        out_shape=jax.ShapeDtypeStruct(parts.shape, jnp.float32),
        compiler_params=params(16),
        name="prefix",
    )(place, parts, inner, other, *totals)
    state = lax.all_to_all(states, exchange, 0, 0, tiled=True).reshape(width, HEAD_DIM)

    return pl.pallas_call(
        final_body,
        in_specs=[VMEM] * 4,
        out_specs=HBM,
        out_shape=jax.ShapeDtypeStruct((rows, width), jnp.bfloat16),
        scratch_shapes=[tokens, pltpu.SemaphoreType.DMA((steps,))],
        compiler_params=params(16),
        name="gated_norm",
    )(queries, inner, scale, state)


def solution(mesh):
    ranges, inner_ranges = mesh.shape["grp"], mesh.shape["seq"]
    bits = inner_ranges.bit_length() - 1
    names = tuple(f"seq{b}" for b in reversed(range(bits)))
    split = Mesh(mesh.devices.reshape((ranges,) + (2,) * bits), ("grp",) + names)
    exchange = tuple(f"seq{b}" for b in EXCHANGE_BITS)
    order = []
    for index in itertools.product(range(2), repeat=bits):
        bit = dict(zip(names, index))
        order.append(sum(bit[name] << (bits - 1 - i) for i, name in enumerate(exchange)))
    rows = P(("grp",) + names, None)
    return jax.shard_map(
        functools.partial(
            per_device, ranges=ranges, inner_ranges=inner_ranges, exchange=exchange, order=tuple(order)
        ),
        mesh=split,
        in_specs=(rows, rows, rows, rows, P()),
        out_specs=rows,
        check_vma=False,
    )
```

```python
import functools
import itertools

import jax
import jax.numpy as jnp
from jax import lax
from jax.experimental import pallas as pl
from jax.experimental.pallas import tpu as pltpu
from jax.sharding import Mesh
from jax.sharding import PartitionSpec as P

HEADS = 8
HEAD_DIM = 128
BLOCK = 256
LANES = 2 * HEAD_DIM
KV_LANES = 4 * HEAD_DIM
EXCHANGE_BITS = (0, 4, 3, 2, 1)


def silu(u):
    half = 0.5 * u.astype(jnp.float32)
    return (half + half * jnp.tanh(half)).astype(jnp.bfloat16)


def dot(a, b, contract):
    return lax.dot_general(a, b, ((contract[0], contract[1]), ((), ())), preferred_element_type=jnp.float32)


def wide_dot(a, state):
    high = state.astype(jnp.bfloat16)
    low = (state - high.astype(jnp.float32)).astype(jnp.bfloat16)
    return dot(jnp.concatenate([a, a], axis=1), jnp.concatenate([high, low], axis=0), ((1,), (0,)))


def stream(sources, targets, sems, lanes):
    pieces = []
    for i in range(sources[0].shape[1] // lanes):
        cols = pl.ds(i * lanes, lanes)
        piece = [
            pltpu.make_async_copy(source.at[:, cols], target.at[:, cols], sem.at[i])
            for source, target, sem in zip(sources, targets, sems)
        ]
        for copy in piece:
            copy.start()
        pieces.append(piece)
    return pieces


def heads_of(i, lanes):
    for h in range(i * lanes // HEAD_DIM, (i + 1) * lanes // HEAD_DIM):
        yield slice(h * HEAD_DIM, (h + 1) * HEAD_DIM)


def blocks_of(rows):
    return [slice(b * BLOCK, (b + 1) * BLOCK) for b in range(rows // BLOCK)]


def kv_body(key_hbm, value_hbm, total_hbm, key_ref, value_ref, total_ref, key_sem, value_sem, total_sem):
    pieces = stream((key_hbm, value_hbm), (key_ref, value_ref), (key_sem, value_sem), KV_LANES)
    stores = []
    for i, piece in enumerate(pieces):
        for copy in piece:
            copy.wait()
        for cols in heads_of(i, KV_LANES):
            total_ref[cols, :] = dot(silu(key_ref[:, cols]), value_ref[:, cols], ((0,), (0,)))
        done = pl.ds(i * KV_LANES, KV_LANES)
        store = pltpu.make_async_copy(total_ref.at[done, :], total_hbm.at[done, :], total_sem.at[i])
        store.start()
        stores.append(store)
    for store in stores:
        store.wait()


def intra_body(
    query_hbm, key_hbm, value_hbm, gate_hbm, gain_ref, queries_ref, inner_ref, scale_ref,
    query_ref, key_ref, value_ref, gate_ref, query_sem, key_sem, value_sem, gate_sem,
):
    pieces = stream(
        (query_hbm, key_hbm, value_hbm, gate_hbm),
        (query_ref, key_ref, value_ref, gate_ref),
        (query_sem, key_sem, value_sem, gate_sem),
        LANES,
    )
    row = lax.broadcasted_iota(jnp.int32, (BLOCK, BLOCK), 0)
    col = lax.broadcasted_iota(jnp.int32, (BLOCK, BLOCK), 1)
    causal = row >= col
    for i, piece in enumerate(pieces):
        for copy in piece:
            copy.wait()
        for cols in heads_of(i, LANES):
            state = None
            for rows in blocks_of(query_hbm.shape[0]):
                q = silu(query_ref[rows, cols])
                k = silu(key_ref[rows, cols])
                v = value_ref[rows, cols]
                queries_ref[rows, cols] = q
                gate = gate_ref[rows, cols].astype(jnp.float32)
                scale_ref[rows, cols] = gain_ref[:, cols] / (1.0 + jnp.exp(-gate))
                scores = jnp.where(causal, dot(q, k, ((1,), (1,))), 0.0).astype(jnp.bfloat16)
                mixed = dot(scores, v, ((1,), (0,)))
                if state is not None:
                    mixed = mixed + wide_dot(q, state)
                inner_ref[rows, cols] = mixed
                if rows.stop < query_hbm.shape[0]:
                    block_kv = dot(k, v, ((0,), (0,)))
                    state = block_kv if state is None else state + block_kv


def final_body(queries_ref, inner_ref, scale_ref, state_ref, out_hbm, out_ref, sem):
    stores = []
    for i in range(queries_ref.shape[1] // LANES):
        for cols in heads_of(i, LANES):
            mixed = inner_ref[:, cols] + wide_dot(queries_ref[:, cols], state_ref[cols, :])
            power = jnp.mean(mixed * mixed, axis=-1, keepdims=True)
            out_ref[:, cols] = (mixed * lax.rsqrt(power + 1e-05) * scale_ref[:, cols]).astype(jnp.bfloat16)
        cols = pl.ds(i * LANES, LANES)
        store = pltpu.make_async_copy(out_ref.at[:, cols], out_hbm.at[:, cols], sem.at[i])
        store.start()
        stores.append(store)
    for store in stores:
        store.wait()


def total_body(part_ref, out_ref):
    total = part_ref[0]
    for m in range(1, part_ref.shape[0]):
        total = total + part_ref[m]
    out_ref[...] = total


def prefix_body(order, place_ref, part_ref, inner_ref, other_ref, *refs):
    del inner_ref
    *total_refs, out_ref = refs
    place = place_ref[0]
    state = jnp.where(place % 2 == 1, other_ref[...], 0.0)
    for pair, total_ref in enumerate(total_refs, 1):
        state = state + jnp.where((place // 2) ^ pair < place // 2, total_ref[...], 0.0)
    for m in order:
        out_ref[m] = state
        if m != order[-1]:
            state = state + part_ref[m]


HBM = pl.BlockSpec(memory_space=pltpu.HBM)
VMEM = pl.BlockSpec(memory_space=pltpu.VMEM)


def params(mib):
    return pltpu.CompilerParams(vmem_limit_bytes=mib * 1024 * 1024)


def per_device(query, key_in, value, gate, gain, ranges, inner_ranges, exchange, order):
    rows, width = query.shape
    steps = width // LANES
    tokens = pltpu.VMEM((rows, width), jnp.bfloat16)
    wide_tokens = pltpu.VMEM((rows, width), jnp.float32)
    sems = pltpu.SemaphoreType.DMA((steps,))
    query, key_in, value, gate = (pltpu.with_memory_space_constraint(a, pltpu.HBM) for a in (query, key_in, value, gate))
    total = pl.pallas_call(
        kv_body,
        in_specs=[HBM, HBM],
        out_specs=HBM,
        out_shape=pltpu.HBM((width, HEAD_DIM), jnp.float32),
        scratch_shapes=[tokens, tokens, pltpu.VMEM((width, HEAD_DIM), jnp.float32)]
        + [pltpu.SemaphoreType.DMA((width // KV_LANES,))] * 3,
        compiler_params=params(16),
        name="range_part",
    )(key_in, value)

    piece = width // inner_ranges
    parts = lax.all_to_all(total.reshape(inner_ranges, piece, HEAD_DIM), exchange, 0, 0, tiled=True)

    queries, inner, scale = pl.pallas_call(
        intra_body,
        in_specs=[HBM, HBM, HBM, HBM, VMEM],
        out_specs=[VMEM] * 3,
        out_shape=[
            jax.ShapeDtypeStruct((rows, width), jnp.bfloat16),
            jax.ShapeDtypeStruct((rows, width), jnp.float32),
            jax.ShapeDtypeStruct((rows, width), jnp.float32),
        ],
        scratch_shapes=[tokens] * 4 + [sems] * 4,
        compiler_params=params(16),
        name="within_block",
    )(query, key_in, value, gate, gain.reshape(1, width))
    parts, queries, inner, scale = lax.optimization_barrier((parts, queries, inner, scale))

    def swap(a, bits):
        return lax.ppermute(a, "grp", [(g, g ^ bits) for g in range(ranges)])

    place = lax.axis_index("grp").astype(jnp.int32).reshape(1)
    range_total = pl.pallas_call(
        total_body,
        in_specs=[VMEM],
        out_specs=VMEM,
        out_shape=jax.ShapeDtypeStruct((piece, HEAD_DIM), jnp.float32),
        compiler_params=params(16),
        name="range_total",
    )(parts)
    other = swap(range_total, 1)
    both = range_total + other
    totals = [swap(both, 2 * pair) for pair in range(1, ranges // 2)]
    states = pl.pallas_call(
        functools.partial(prefix_body, order),
        in_specs=[pl.BlockSpec(memory_space=pltpu.SMEM)] + [VMEM] * (3 + len(totals)),
        out_specs=VMEM,
        out_shape=jax.ShapeDtypeStruct(parts.shape, jnp.float32),
        compiler_params=params(16),
        name="prefix",
    )(place, parts, inner, other, *totals)
    state = lax.all_to_all(states, exchange, 0, 0, tiled=True).reshape(width, HEAD_DIM)

    return pl.pallas_call(
        final_body,
        in_specs=[VMEM] * 4,
        out_specs=HBM,
        out_shape=jax.ShapeDtypeStruct((rows, width), jnp.bfloat16),
        scratch_shapes=[tokens, pltpu.SemaphoreType.DMA((steps,))],
        compiler_params=params(16),
        name="gated_norm",
    )(queries, inner, scale, state)


def solution(mesh):
    ranges, inner_ranges = mesh.shape["grp"], mesh.shape["seq"]
    bits = inner_ranges.bit_length() - 1
    names = tuple(f"seq{b}" for b in reversed(range(bits)))
    split = Mesh(mesh.devices.reshape((ranges,) + (2,) * bits), ("grp",) + names)
    exchange = tuple(f"seq{b}" for b in EXCHANGE_BITS)
    order = []
    for index in itertools.product(range(2), repeat=bits):
        bit = dict(zip(names, index))
        order.append(sum(bit[name] << (bits - 1 - i) for i, name in enumerate(exchange)))
    rows = P(("grp",) + names, None)
    return jax.shard_map(
        functools.partial(
            per_device, ranges=ranges, inner_ranges=inner_ranges, exchange=exchange, order=tuple(order)
        ),
        mesh=split,
        in_specs=(rows, rows, rows, rows, P()),
        out_specs=rows,
        check_vma=False,
    )
```

```python
import functools
import itertools

import jax
import jax.numpy as jnp
from jax import lax
from jax.experimental import pallas as pl
from jax.experimental.pallas import tpu as pltpu
from jax.sharding import Mesh
from jax.sharding import PartitionSpec as P

HEADS = 8
HEAD_DIM = 128
BLOCK = 256
LANES = 2 * HEAD_DIM
KV_LANES = 4 * HEAD_DIM
EXCHANGE_BITS = (0, 4, 2, 3, 1)


def silu(u):
    half = 0.5 * u.astype(jnp.float32)
    return (half + half * jnp.tanh(half)).astype(jnp.bfloat16)


def dot(a, b, contract):
    return lax.dot_general(a, b, ((contract[0], contract[1]), ((), ())), preferred_element_type=jnp.float32)


def wide_dot(a, state):
    high = state.astype(jnp.bfloat16)
    low = (state - high.astype(jnp.float32)).astype(jnp.bfloat16)
    return dot(jnp.concatenate([a, a], axis=1), jnp.concatenate([high, low], axis=0), ((1,), (0,)))


def stream(sources, targets, sems, lanes):
    pieces = []
    for i in range(sources[0].shape[1] // lanes):
        cols = pl.ds(i * lanes, lanes)
        piece = [
            pltpu.make_async_copy(source.at[:, cols], target.at[:, cols], sem.at[i])
            for source, target, sem in zip(sources, targets, sems)
        ]
        for copy in piece:
            copy.start()
        pieces.append(piece)
    return pieces


def heads_of(i, lanes):
    for h in range(i * lanes // HEAD_DIM, (i + 1) * lanes // HEAD_DIM):
        yield slice(h * HEAD_DIM, (h + 1) * HEAD_DIM)


def blocks_of(rows):
    return [slice(b * BLOCK, (b + 1) * BLOCK) for b in range(rows // BLOCK)]


def kv_body(key_hbm, value_hbm, total_hbm, key_ref, value_ref, total_ref, key_sem, value_sem, total_sem):
    pieces = stream((key_hbm, value_hbm), (key_ref, value_ref), (key_sem, value_sem), KV_LANES)
    stores = []
    for i, piece in enumerate(pieces):
        for copy in piece:
            copy.wait()
        for cols in heads_of(i, KV_LANES):
            total_ref[cols, :] = dot(silu(key_ref[:, cols]), value_ref[:, cols], ((0,), (0,)))
        done = pl.ds(i * KV_LANES, KV_LANES)
        store = pltpu.make_async_copy(total_ref.at[done, :], total_hbm.at[done, :], total_sem.at[i])
        store.start()
        stores.append(store)
    for store in stores:
        store.wait()


def intra_body(
    query_hbm, key_hbm, value_hbm, gate_hbm, gain_ref, queries_ref, inner_ref, scale_ref,
    query_ref, key_ref, value_ref, gate_ref, query_sem, key_sem, value_sem, gate_sem,
):
    pieces = stream(
        (query_hbm, key_hbm, value_hbm, gate_hbm),
        (query_ref, key_ref, value_ref, gate_ref),
        (query_sem, key_sem, value_sem, gate_sem),
        LANES,
    )
    row = lax.broadcasted_iota(jnp.int32, (BLOCK, BLOCK), 0)
    col = lax.broadcasted_iota(jnp.int32, (BLOCK, BLOCK), 1)
    causal = row >= col
    for i, piece in enumerate(pieces):
        for copy in piece:
            copy.wait()
        for cols in heads_of(i, LANES):
            state = None
            for rows in blocks_of(query_hbm.shape[0]):
                q = silu(query_ref[rows, cols])
                k = silu(key_ref[rows, cols])
                v = value_ref[rows, cols]
                queries_ref[rows, cols] = q
                gate = gate_ref[rows, cols].astype(jnp.float32)
                scale_ref[rows, cols] = gain_ref[:, cols] / (1.0 + jnp.exp(-gate))
                scores = jnp.where(causal, dot(q, k, ((1,), (1,))), 0.0).astype(jnp.bfloat16)
                mixed = dot(scores, v, ((1,), (0,)))
                if state is not None:
                    mixed = mixed + wide_dot(q, state)
                inner_ref[rows, cols] = mixed
                if rows.stop < query_hbm.shape[0]:
                    block_kv = dot(k, v, ((0,), (0,)))
                    state = block_kv if state is None else state + block_kv


def final_body(queries_ref, inner_ref, scale_ref, state_ref, out_hbm, out_ref, sem):
    stores = []
    for i in range(queries_ref.shape[1] // LANES):
        for cols in heads_of(i, LANES):
            mixed = inner_ref[:, cols] + wide_dot(queries_ref[:, cols], state_ref[cols, :])
            power = jnp.mean(mixed * mixed, axis=-1, keepdims=True)
            out_ref[:, cols] = (mixed * lax.rsqrt(power + 1e-05) * scale_ref[:, cols]).astype(jnp.bfloat16)
        cols = pl.ds(i * LANES, LANES)
        store = pltpu.make_async_copy(out_ref.at[:, cols], out_hbm.at[:, cols], sem.at[i])
        store.start()
        stores.append(store)
    for store in stores:
        store.wait()


def total_body(part_ref, out_ref):
    total = part_ref[0]
    for m in range(1, part_ref.shape[0]):
        total = total + part_ref[m]
    out_ref[...] = total


def prefix_body(order, place_ref, part_ref, inner_ref, other_ref, *refs):
    del inner_ref
    *total_refs, out_ref = refs
    place = place_ref[0]
    state = jnp.where(place % 2 == 1, other_ref[...], 0.0)
    for pair, total_ref in enumerate(total_refs, 1):
        state = state + jnp.where((place // 2) ^ pair < place // 2, total_ref[...], 0.0)
    for m in order:
        out_ref[m] = state
        if m != order[-1]:
            state = state + part_ref[m]


HBM = pl.BlockSpec(memory_space=pltpu.HBM)
VMEM = pl.BlockSpec(memory_space=pltpu.VMEM)


def params(mib):
    return pltpu.CompilerParams(vmem_limit_bytes=mib * 1024 * 1024)


def per_device(query, key_in, value, gate, gain, ranges, inner_ranges, exchange, order):
    rows, width = query.shape
    steps = width // LANES
    tokens = pltpu.VMEM((rows, width), jnp.bfloat16)
    wide_tokens = pltpu.VMEM((rows, width), jnp.float32)
    sems = pltpu.SemaphoreType.DMA((steps,))
    query, key_in, value, gate = (pltpu.with_memory_space_constraint(a, pltpu.HBM) for a in (query, key_in, value, gate))
    total = pl.pallas_call(
        kv_body,
        in_specs=[HBM, HBM],
        out_specs=HBM,
        out_shape=pltpu.HBM((width, HEAD_DIM), jnp.float32),
        scratch_shapes=[tokens, tokens, pltpu.VMEM((width, HEAD_DIM), jnp.float32)]
        + [pltpu.SemaphoreType.DMA((width // KV_LANES,))] * 3,
        compiler_params=params(16),
        name="range_part",
    )(key_in, value)

    piece = width // inner_ranges
    parts = lax.all_to_all(total.reshape(inner_ranges, piece, HEAD_DIM), exchange, 0, 0, tiled=True)

    queries, inner, scale = pl.pallas_call(
        intra_body,
        in_specs=[HBM, HBM, HBM, HBM, VMEM],
        out_specs=[VMEM] * 3,
        out_shape=[
            jax.ShapeDtypeStruct((rows, width), jnp.bfloat16),
            jax.ShapeDtypeStruct((rows, width), jnp.float32),
            jax.ShapeDtypeStruct((rows, width), jnp.float32),
        ],
        scratch_shapes=[tokens] * 4 + [sems] * 4,
        compiler_params=params(16),
        name="within_block",
    )(query, key_in, value, gate, gain.reshape(1, width))
    parts, queries, inner, scale = lax.optimization_barrier((parts, queries, inner, scale))

    def swap(a, bits):
        return lax.ppermute(a, "grp", [(g, g ^ bits) for g in range(ranges)])

    place = lax.axis_index("grp").astype(jnp.int32).reshape(1)
    range_total = pl.pallas_call(
        total_body,
        in_specs=[VMEM],
        out_specs=VMEM,
        out_shape=jax.ShapeDtypeStruct((piece, HEAD_DIM), jnp.float32),
        compiler_params=params(16),
        name="range_total",
    )(parts)
    other = swap(range_total, 1)
    both = range_total + other
    totals = [swap(both, 2 * pair) for pair in range(1, ranges // 2)]
    states = pl.pallas_call(
        functools.partial(prefix_body, order),
        in_specs=[pl.BlockSpec(memory_space=pltpu.SMEM)] + [VMEM] * (3 + len(totals)),
        out_specs=VMEM,
        out_shape=jax.ShapeDtypeStruct(parts.shape, jnp.float32),
        compiler_params=params(16),
        name="prefix",
    )(place, parts, inner, other, *totals)
    state = lax.all_to_all(states, exchange, 0, 0, tiled=True).reshape(width, HEAD_DIM)

    return pl.pallas_call(
        final_body,
        in_specs=[VMEM] * 4,
        out_specs=HBM,
        out_shape=jax.ShapeDtypeStruct((rows, width), jnp.bfloat16),
        scratch_shapes=[tokens, pltpu.SemaphoreType.DMA((steps,))],
        compiler_params=params(16),
        name="gated_norm",
    )(queries, inner, scale, state)


def solution(mesh):
    ranges, inner_ranges = mesh.shape["grp"], mesh.shape["seq"]
    bits = inner_ranges.bit_length() - 1
    names = tuple(f"seq{b}" for b in reversed(range(bits)))
    split = Mesh(mesh.devices.reshape((ranges,) + (2,) * bits), ("grp",) + names)
    exchange = tuple(f"seq{b}" for b in EXCHANGE_BITS)
    order = []
    for index in itertools.product(range(2), repeat=bits):
        bit = dict(zip(names, index))
        order.append(sum(bit[name] << (bits - 1 - i) for i, name in enumerate(exchange)))
    rows = P(("grp",) + names, None)
    return jax.shard_map(
        functools.partial(
            per_device, ranges=ranges, inner_ranges=inner_ranges, exchange=exchange, order=tuple(order)
        ),
        mesh=split,
        in_specs=(rows, rows, rows, rows, P()),
        out_specs=rows,
        check_vma=False,
    )
```
